32 devices in a mesh: groups: 2 (over y), tensor: 4 (over z), section: 4 (over x, core).
Axes of the slice: x: 2, y: 2, z: 4, core: 2. Of those that a mesh axis runs over, the one named last changes fastest.
Arguments:
- hidden: bfloat16 [16, 8192], P('groups', 'tensor'), parts along dimension 0, may hold values from -6 to 6
- norm_gain: bfloat16 [4, 8192], P('section'), may hold values from 0.5 to 1.5
- query_weight: bfloat16 [4, 8192, 512], P('section', None, 'tensor'), may hold values from -0.0625 to 0.0625
- query_bias: bfloat16 [4, 512], P('section', 'tensor'), may hold values from -10 to 10
- kv_weight: bfloat16 [4, 8192, 1024], P('section', None, 'tensor'), may hold values from -0.0625 to 0.0625
- out_weight: bfloat16 [4, 512, 8192], P('section', None, 'tensor'), may hold values from -0.25 to 0.25
- kv_pool: bfloat16 [4, 48, 16, 1024], P('section', ('groups', 'tensor')), parts along dimension 1, may hold values from -8 to 8
- page_table: int32 [16, 4], P(('groups', 'tensor')), parts along dimension 0, may hold values from 0 to 23, as said below
- context_len: int32 [16], P(('groups', 'tensor')), parts along dimension 0, may hold values from 33 to 64, as said below
Outputs:
- result: bfloat16 [16, 8192], P(('groups', 'section'), 'tensor'), parts along dimension 0
The draws below stay inside these ranges and needn't reach their ends.
There are 2 independent parts, one for each index of `groups`. The reference program is written for one: setup_inputs(seed, part) draws one part's arguments, and reference() takes and returns one part's arrays. A program takes and returns all parts, laid end to end along the dimension named above; an argument that names none is the same for every part. Nothing has to cross between parts.
Inputs may be any that keep to these rules, and one draw needn't show every extreme that they name: `page_table`: sample r belongs to block k = r // 2; its 4 pages lie in k * 6 to (k + 1) * 6 - 1. The first 2 pages are the same for all samples of a block, every other page belongs to one sample only. `context_len`: some sample has 64 cached tokens.
All inputs are finite; a program needn't handle non-finite values.
Results may differ from the reference program's by a relative error of at most 0.018.
Values may be sent and summed in bfloat16 or wider, within the bound.
No kernel may reach another device: no remote copies, remote signals or barrier semaphores. Data moves between devices by JAX's collectives and lax.ppermute only.
A program may use at most 64 MiB of HBM per device.

```python
import jax
import jax.numpy as jnp
from jax import lax

D = 8192
HD = 128
HEADS = 4
KVH = 4
LAYERS = 4
ROW_DEV = 2
ROWS = 8
PAGE_LEN = 16
BLOCKS = 4
PREFIX_BLOCKS = 2
CTX = 64
POOL_DEV = 6
PAGES = 24
N_TENSOR = 4


def device_order(sub_key):
    return jax.random.permutation(sub_key, POOL_DEV).astype(jnp.int32)


def draw_page_table(key, part):
    orders = jax.vmap(device_order)(jax.random.split(jax.random.fold_in(key, 11), N_TENSOR))
    shared = jnp.broadcast_to(orders[:, None, :PREFIX_BLOCKS], (N_TENSOR, ROW_DEV, PREFIX_BLOCKS))
    private = orders[:, PREFIX_BLOCKS:].reshape(N_TENSOR, ROW_DEV, BLOCKS - PREFIX_BLOCKS)
    offsets = (jnp.arange(N_TENSOR, dtype=jnp.int32) * POOL_DEV)[:, None, None]
    table = jnp.concatenate([shared, private], axis=2) + offsets
    return table.reshape(ROWS, BLOCKS).astype(jnp.int32)


def draw_context_len(key, part):
    lowest = PREFIX_BLOCKS * PAGE_LEN + 1
    highest = BLOCKS * PAGE_LEN
    drawn = jax.random.randint(jax.random.fold_in(key, 23), (ROWS,), lowest, highest + 1, dtype=jnp.int32)
    marked = jax.random.randint(jax.random.fold_in(key, 29), (), 0, ROWS, dtype=jnp.int32)
    return jnp.where(jnp.arange(ROWS, dtype=jnp.int32) == marked, highest, drawn).astype(jnp.int32)


def draw_kv_pool(key, part):
    shape = (LAYERS, PAGES, PAGE_LEN, 2 * KVH * HD)
    base = jnp.clip(jax.random.normal(jax.random.fold_in(key, 31), shape, jnp.float32), -6.0, 6.0)
    return base.astype(jnp.bfloat16)


def draw_query_bias(key, part):
    shape = (LAYERS, HEADS * HD)
    base = jnp.clip(jax.random.normal(jax.random.fold_in(key, 43), shape, jnp.float32), -4.0, 4.0)
    return base.astype(jnp.bfloat16)


def level_of(rng, extent, shards, low, high):
    level, own = 1.0, jax.random.fold_in(rng, 6)
    for dim, parts in shards:
        steps = jnp.exp(jax.random.uniform(jax.random.fold_in(own, dim), (parts,), jnp.float32, low / len(shards), high / len(shards)))
        level = level * jnp.repeat(steps, extent[dim] // parts).reshape([-1 if axis == dim else 1 for axis in range(len(extent))])
    return level


def normal_values(key, extent, width, most, cuts=(), kind=jnp.bfloat16):
    level = level_of(key, extent, cuts, -0.22, 0.18) if cuts else 1.0
    values = jax.random.normal(key, extent, jnp.float32) * width * level
    return jnp.minimum(jnp.maximum(values, -most), most).astype(kind)


def setup_inputs(seed: int = 0, part: int = 0) -> dict:
    arg_keys = jax.random.split(jax.random.key(seed), 10)
    part_splits = jax.random.split(jax.random.fold_in(arg_keys[9], part), 10)
    return {
        "hidden": normal_values(part_splits[0], (ROWS, D), 1.0, 6.0, ((1, 4),)),
        "norm_gain": jnp.clip(1.0 + 0.1 * jax.random.normal(arg_keys[1], (LAYERS, D), jnp.float32), 0.5, 1.5).astype(jnp.bfloat16),
        "query_weight": normal_values(arg_keys[2], (LAYERS, D, HEADS * HD), D ** -0.5, 0.0625, ((0, 4), (2, 4))),
        "query_bias": draw_query_bias(jax.random.fold_in(arg_keys[9], 71), part),
        "kv_weight": normal_values(arg_keys[4], (LAYERS, D, 2 * KVH * HD), D ** -0.5, 0.0625, ((0, 4), (2, 4))),
        "out_weight": normal_values(arg_keys[5], (LAYERS, HEADS * HD, D), (HEADS * HD) ** -0.5, 0.25, ((0, 4), (2, 4))),
        "kv_pool": draw_kv_pool(jax.random.fold_in(jax.random.fold_in(arg_keys[9], part), 71), part),
        "page_table": draw_page_table(jax.random.fold_in(jax.random.fold_in(arg_keys[9], part), 71), part),
        "context_len": draw_context_len(jax.random.fold_in(jax.random.fold_in(arg_keys[9], part), 71), part),
    }


epsilon = 1e-06
rope_base = 1000000.0

def rotate(values, position):
    head_size = values.shape[-1]
    half_size = head_size // 2
    frequency = rope_base ** (-(jnp.arange(half_size, dtype=jnp.float32) * 2.0) / head_size)
    angles = position.astype(jnp.float32)[:, None] * frequency[None, :]
    cosine = jnp.cos(angles)[:, None, :]
    sine_part = jnp.sin(angles)[:, None, :]
    front_half = values[..., :half_size]
    back_half = values[..., half_size:]
    return jnp.concatenate([front_half * cosine - back_half * sine_part, back_half * cosine + front_half * sine_part], axis=-1)

def attend(queries, key_new, value_new, cached, position):
    row_count, head_count, head_size = queries.shape
    kv_heads = key_new.shape[1]
    group_size = head_count // kv_heads
    span_len = cached.shape[1]
    keys_all = cached[:, :, :kv_heads * head_size].reshape(row_count, span_len, kv_heads, head_size).astype(jnp.float32)
    values_all = cached[:, :, kv_heads * head_size:].reshape(row_count, span_len, kv_heads, head_size).astype(jnp.float32)
    grouped = queries.reshape(row_count, kv_heads, group_size, head_size).astype(jnp.float32)
    scaling = head_size ** (-0.5)
    scores = jnp.einsum('rkgd,rskd->rkgs', grouped, keys_all) * scaling
    own_score = jnp.einsum('rkgd,rkd->rkg', grouped, key_new.astype(jnp.float32)) * scaling
    usable = (jnp.arange(span_len, dtype=jnp.int32)[None, :] < position[:, None])[:, None, None, :]
    row_max = jnp.maximum(lax.optimization_barrier(jnp.max(jnp.where(usable, scores, -1e+30), axis=-1)), own_score)
    weights = jnp.where(usable, jnp.exp(scores - row_max[..., None]), 0.0)
    own_weight = jnp.exp(own_score - row_max)
    denominator = lax.optimization_barrier(jnp.sum(weights, axis=-1)) + own_weight
    weights = (weights / denominator[..., None]).astype(jnp.bfloat16)
    own_weight = (own_weight / denominator).astype(jnp.bfloat16)
    mixture = jnp.einsum('rkgs,rskd->rkgd', weights.astype(jnp.float32), values_all)
    mixture = mixture + own_weight.astype(jnp.float32)[..., None] * value_new.astype(jnp.float32)[:, :, None, :]
    return mixture.reshape(row_count, head_count * head_size).astype(jnp.bfloat16)

def reference(hidden, norm_gain, query_weight, query_bias, kv_weight, out_weight, kv_pool, page_table, context_len):
    stream = hidden
    for layer_index in range(LAYERS):
        wide_rows = stream.astype(jnp.float32)
        mean_sq = lax.optimization_barrier(jnp.mean(wide_rows * wide_rows, axis=1, keepdims=True))
        normed = (wide_rows * lax.rsqrt(mean_sq + epsilon) * norm_gain[layer_index].astype(jnp.float32)).astype(jnp.bfloat16)
        queries = (jnp.dot(normed, query_weight[layer_index], preferred_element_type=jnp.float32) + query_bias[layer_index].astype(jnp.float32)).astype(jnp.bfloat16)
        fresh_kv = jnp.dot(normed, kv_weight[layer_index], preferred_element_type=jnp.float32).astype(jnp.bfloat16)
        cached = kv_pool[layer_index][page_table].reshape(ROWS, CTX, 2 * KVH * HD)
        rotated = rotate(queries.reshape(ROWS, HEADS, HD).astype(jnp.float32), context_len).astype(jnp.bfloat16)
        key_new = rotate(fresh_kv[:, :KVH * HD].reshape(ROWS, KVH, HD).astype(jnp.float32), context_len).astype(jnp.bfloat16)
        value_new = fresh_kv[:, KVH * HD:].reshape(ROWS, KVH, HD)
        mixture = attend(rotated, key_new, value_new, cached, context_len)
        stream = (wide_rows + jnp.dot(mixture, out_weight[layer_index], preferred_element_type=jnp.float32)).astype(jnp.bfloat16)
    return stream
```

```python
import functools

import jax
import jax.numpy as jnp
from jax import lax
from jax.experimental import pallas as pl
from jax.experimental.pallas import tpu as pltpu
from jax.sharding import PartitionSpec as P

HD = 128
epsilon = 1e-06
rope_base = 1000000.0
DIRECT_PEERS = 8
VMEM = pl.BlockSpec(memory_space=pltpu.VMEM)
SMEM = pl.BlockSpec(memory_space=pltpu.SMEM)


def round_up(value, unit):
    return -(-value // unit) * unit


def kernel_call(body, outs, in_specs, scratch=(), many=True):
    specs = [VMEM] * len(outs)
    return pl.pallas_call(
        body,
        out_shape=outs if many else outs[0],
        in_specs=in_specs,
        out_specs=specs if many else specs[0],
        scratch_shapes=list(scratch),
    )


class Ring:
    def __init__(self):
        self.count = lax.axis_size("tensor")
        self.sections = lax.axis_size("section")
        self.direct = self.count <= DIRECT_PEERS
        me = lax.axis_index("tensor")
        order = jnp.arange(self.count, dtype=jnp.int32)
        self.sources = (me - order) % self.count if self.direct else order
        self.targets = (me + order) % self.count if self.direct else order

    def send(self, value, pairs, step):
        n = self.count
        m = self.sections
        perm = [(t * m + a, (t + step) % n * m + b) for a, b in pairs for t in range(n)]
        return lax.ppermute(value, ("tensor", "section"), perm)

    def gather(self, value, origin, target):
        if self.direct:
            got = [] if origin != target else [value]
            first = len(got)
            return got + [
                self.send(value, [(origin, target)], step) for step in range(first, self.count)
            ]
        if origin != target:
            value = lax.ppermute(value, "section", [(origin, target)])
        whole = lax.all_gather(value, "tensor", axis=0, tiled=False)
        return [whole[slot] for slot in range(self.count)]

    def trade(self, values):
        if self.direct:
            every = [(s, s) for s in range(self.sections)]
            return [values[0]] + [
                self.send(values[step], every, step) for step in range(1, self.count)
            ]
        swapped = lax.all_to_all(
            jnp.stack(values), "tensor", split_axis=0, concat_axis=0, tiled=True
        )
        return [swapped[slot] for slot in range(self.count)]


def pack_kernel(info, tensor_ref, targets, table, context, pool, *outs):
    n, heads_dev, group, kv_heads, width, page_len = info
    tokens = pool.shape[0]
    pages = tokens // page_len
    row_dev, blocks = table.shape
    extra = outs[0].shape[0] - tokens
    lane = lax.broadcasted_iota(jnp.int32, (extra, 2 * width), 1)
    row = lax.broadcasted_iota(jnp.int32, (extra, 2 * width), 0)
    first = tensor_ref[0] * pages
    aux = jnp.zeros((extra, 2 * width), jnp.float32)
    for j in range(row_dev):
        length = context[j]
        uses = jnp.zeros((extra, 2 * width), jnp.float32)
        for b in range(blocks):
            offset = lane - (table[j, b] - first) * page_len
            inside = (offset >= 0) & (offset < page_len) & (offset + b * page_len < length)
            uses = uses + jnp.where(inside, 1.0, 0.0)
        aux = jnp.where(row == j, uses, aux)
        aux = jnp.where(row == row_dev + j, length.astype(jnp.float32), aux)
    aux = aux.astype(jnp.bfloat16)
    for k in range(n):
        head = (targets[k] * heads_dev) // group * HD
        key_at = pl.multiple_of(head, HD)
        value_at = pl.multiple_of(head + kv_heads * HD, HD)
        outs[k][0:tokens, 0:width] = pool[:, pl.ds(key_at, width)]
        outs[k][0:tokens, width : 2 * width] = pool[:, pl.ds(value_at, width)]
        outs[k][tokens:, :] = aux


def unpack_kernel(info, sources, frequency, *refs):
    n, row_dev, tokens = info
    packs = refs[:n]
    counts, cosine, sine, lengths = refs[n:]
    counts[...] = jnp.zeros_like(counts)
    for k in range(n):
        aux = packs[k][tokens:, :].astype(jnp.float32)
        base = sources[k] * row_dev
        for j in range(row_dev):
            counts[k, pl.ds(base + j, 1), :] = aux[j : j + 1, :tokens]
            lengths[pl.ds(base + j, 1), :] = aux[row_dev + j : row_dev + j + 1, :HD]
    angles = lengths[...] * frequency[...]
    lane = lax.broadcasted_iota(jnp.int32, angles.shape, 1)
    cosine[...] = jnp.cos(angles)
    sine[...] = jnp.where(lane < HD // 2, -1.0, 1.0) * jnp.sin(angles)


def rotate(values, cosine, sine):
    swapped = jnp.concatenate([values[:, HD // 2 :], values[:, : HD // 2]], axis=1)
    return values * cosine + swapped * sine


def project_kernel(info, sources, gain, wq, wkv, bias, counts, cosine, sine, *refs):
    n, heads_dev, group, tokens, width = info
    pieces = refs[:n]
    packs = refs[n : 2 * n]
    out = refs[2 * n]
    slice_len = pieces[0].shape[1]
    features = n * slice_len
    wide = [piece[...].astype(jnp.float32) for piece in pieces]
    total = functools.reduce(
        jnp.add, [jnp.sum(value * value, axis=1, keepdims=True) for value in wide]
    )
    inverse = lax.rsqrt(total * (1.0 / features) + epsilon)
    queries = None
    for k in range(n):
        at = pl.multiple_of(sources[k] * slice_len, HD)
        scale = gain[:, pl.ds(at, slice_len)].astype(jnp.float32)
        normed = (wide[k] * inverse * scale).astype(jnp.bfloat16)
        q_part = jnp.dot(normed, wq[pl.ds(at, slice_len), :], preferred_element_type=jnp.float32)
        kv_part = jnp.dot(normed, wkv[pl.ds(at, slice_len), :], preferred_element_type=jnp.float32)
        queries = q_part if queries is None else queries + q_part
        fresh = kv_part if k == 0 else fresh + kv_part
    queries = (queries + bias[...].astype(jnp.float32)).astype(jnp.bfloat16).astype(jnp.float32)
    span = heads_dev * HD
    out[:, 3 * span : 3 * span + fresh.shape[1]] = fresh.astype(jnp.bfloat16).astype(jnp.float32)
    for i in range(heads_dev):
        head = slice(i * HD, (i + 1) * HD)
        rotated = rotate(queries[:, head], cosine[...], sine[...]).astype(jnp.bfloat16)
        key_at = (i // group) * HD
        scores = []
        for k in range(n):
            keys = packs[k][0:tokens, key_at : key_at + HD]
            scores.append(
                lax.dot_general(
                    rotated, keys, (((1,), (1,)), ((), ())), preferred_element_type=jnp.float32
                )
                * HD ** (-0.5)
            )
        tops = [
            jnp.where(counts[k] > 0.0, scores[k], -1e30) for k in range(n)
        ]
        top = functools.reduce(
            jnp.maximum, [jnp.max(value, axis=1, keepdims=True) for value in tops]
        )
        mass = 0.0
        mixed = 0.0
        for k in range(n):
            weight = counts[k] * jnp.exp(tops[k] - top)
            mass = mass + jnp.sum(weight, axis=1, keepdims=True)
            values = packs[k][0:tokens, width + key_at : width + key_at + HD]
            mixed = mixed + jnp.dot(
                weight.astype(jnp.bfloat16), values, preferred_element_type=jnp.float32
            )
        out[:, i * HD : (i + 1) * HD] = rotated.astype(jnp.float32)
        out[:, span + i * HD : span + (i + 1) * HD] = mixed / mass
        out[:, 2 * span + i * HD : 2 * span + (i + 1) * HD] = jnp.broadcast_to(
            top + jnp.log(mass), (mixed.shape[0], HD)
        )


def output_kernel(info, sources, own, wout, cosine, sine, *refs):
    n, heads_dev, group, kv_heads, kv_width, splits = info
    parts = refs[:n]
    outs = refs[n : n + splits]
    slots, fresh = refs[n + splits :]
    span = heads_dev * HD
    for k in range(n):
        slots[sources[k]] = parts[k][...]
    for j in range(n):
        fresh[:, j * kv_width : (j + 1) * kv_width] = slots[j, :, 3 * span : 3 * span + kv_width]
    keys = []
    for h in range(kv_heads):
        key = rotate(fresh[:, h * HD : (h + 1) * HD], cosine[...], sine[...])
        keys.append(key.astype(jnp.bfloat16).astype(jnp.float32))
    mixture = []
    for h in range(n * heads_dev):
        j, i = divmod(h, heads_dev)
        kv = h // group
        query = slots[j, :, i * HD : (i + 1) * HD]
        cached = slots[j, :, span + i * HD : span + (i + 1) * HD]
        level = slots[j, :, 2 * span + i * HD : 2 * span + (i + 1) * HD]
        value = fresh[:, (kv_heads + kv) * HD : (kv_heads + kv + 1) * HD]
        score = jnp.sum(query * keys[kv], axis=1, keepdims=True) * HD ** (-0.5)
        weight = 1.0 / (1.0 + jnp.exp(level - score))
        mixture.append((cached + weight * (value - cached)).astype(jnp.bfloat16))
    mixture = jnp.concatenate(mixture, axis=1)
    stream = own[...].astype(jnp.float32) + jnp.dot(
        mixture, wout[...], preferred_element_type=jnp.float32
    )
    stream = stream.astype(jnp.bfloat16)
    rows = stream.shape[0] // splits
    for part in range(splits):
        outs[part][...] = stream[part * rows : (part + 1) * rows]


def shards(
    hidden,
    norm_gain,
    query_weight,
    query_bias,
    kv_weight,
    out_weight,
    kv_pool,
    page_table,
    context_len,
):
    ring = Ring()
    n = ring.count
    sections = ring.sections
    section_id = lax.axis_index("section")
    tensor_id = lax.axis_index("tensor")
    rows, slice_len = hidden.shape
    row_dev = page_table.shape[0]
    page_len = kv_pool.shape[2]
    tokens = kv_pool.shape[1] * page_len
    wq, wkv, wout = query_weight[0], kv_weight[0], out_weight[0]
    heads_dev = wq.shape[1] // HD
    kv_width = wkv.shape[1]
    kv_heads = kv_pool.shape[3] // (2 * HD)
    group = heads_dev * n // kv_heads
    width = max(1, heads_dev // group) * HD
    f32, bf16 = jnp.float32, jnp.bfloat16

    pieces = ring.gather(hidden, 0, 0)

    extra = round_up(2 * row_dev, 16)
    pack_info = (n, heads_dev, group, kv_heads, width, page_len)
    packs = kernel_call(
        functools.partial(pack_kernel, pack_info),
        [jax.ShapeDtypeStruct((tokens + extra, 2 * width), bf16)] * n,
        [SMEM] * 4 + [VMEM],
    )(
        tensor_id.reshape(1),
        ring.targets,
        page_table,
        context_len,
        kv_pool.reshape(tokens, kv_pool.shape[3]),
    )
    packs = ring.trade(packs)
    frequency = rope_base ** (-(jnp.arange(HD // 2, dtype=f32) * 2.0) / HD)
    frequency = jnp.concatenate([frequency, frequency])[None, :]
    counts, cosine, sine = kernel_call(
        functools.partial(unpack_kernel, (n, row_dev, tokens)),
        [
            jax.ShapeDtypeStruct((n, rows, tokens), f32),
            jax.ShapeDtypeStruct((rows, HD), f32),
            jax.ShapeDtypeStruct((rows, HD), f32),
        ],
        [SMEM, VMEM] + [VMEM] * n,
        [pltpu.VMEM((rows, HD), f32)],
    )(ring.sources, frequency, *packs)

    message = 3 * heads_dev * HD + round_up(kv_width, HD)
    project = kernel_call(
        functools.partial(project_kernel, (n, heads_dev, group, tokens, width)),
        [jax.ShapeDtypeStruct((rows, message), f32)],
        [SMEM] + [VMEM] * (7 + 2 * n),
        many=False,
    )
    for layer in range(sections):
        sent = project(
            ring.sources, norm_gain, wq, wkv, query_bias, counts, cosine, sine, *pieces, *packs
        )
        parts = ring.gather(sent, layer, layer)
        splits = sections if layer == sections - 1 else 1
        own = pieces[0] if ring.direct else pieces_own(pieces, tensor_id)
        stream = kernel_call(
            functools.partial(
                output_kernel, (n, heads_dev, group, kv_heads, kv_width, splits)
            ),
            [jax.ShapeDtypeStruct((rows // splits, slice_len), bf16)] * splits,
            [SMEM] + [VMEM] * (4 + n),
            [pltpu.VMEM((n, rows, message), f32), pltpu.VMEM((rows, n * kv_width), f32)],
        )(ring.sources, own, wout, cosine, sine, *parts)
        if layer < sections - 1:
            pieces = ring.gather(stream[0], layer, layer + 1)
    last = sections - 1
    result = jnp.where(section_id == last, stream[last], jnp.zeros_like(stream[last]))
    for target in range(last):
        result = result + lax.ppermute(stream[target], "section", [(last, target)])
    return result


def pieces_own(pieces, tensor_id):
    return lax.dynamic_index_in_dim(jnp.stack(pieces), tensor_id, 0, keepdims=False)


def solution(mesh):
    return jax.shard_map(
        shards,
        mesh=mesh,
        in_specs=(
            P("groups", "tensor"),
            P("section", None),
            P("section", None, "tensor"),
            P("section", "tensor"),
            P("section", None, "tensor"),
            P("section", None, "tensor"),
            P("section", ("groups", "tensor"), None, None),
            P(("groups", "tensor"), None),
            P(("groups", "tensor")),
        ),
        out_specs=P(("groups", "section"), "tensor"),
        check_vma=False,
    )
```

```python
import functools

import jax
import jax.numpy as jnp
from jax import lax
from jax.experimental import pallas as pl
from jax.experimental.pallas import tpu as pltpu
from jax.sharding import PartitionSpec as P

HD = 128
epsilon = 1e-06
rope_base = 1000000.0
DIRECT_PEERS = 8
KERNEL_VMEM = 24 * 2**20
VMEM = pl.BlockSpec(memory_space=pltpu.VMEM)
SMEM = pl.BlockSpec(memory_space=pltpu.SMEM)


def round_up(value, unit):
    return -(-value // unit) * unit


def kernel_call(body, outs, in_specs, scratch=(), many=True):
    specs = [VMEM] * len(outs)
    call = pl.pallas_call(
        body,
        out_shape=outs if many else outs[0],
        in_specs=in_specs,
        out_specs=specs if many else specs[0],
        scratch_shapes=list(scratch),
        compiler_params=pltpu.CompilerParams(vmem_limit_bytes=KERNEL_VMEM),
    )

    def placed(*operands):
        return call(
            *[
                pltpu.with_memory_space_constraint(value, pltpu.VMEM) if spec is VMEM else value
                for value, spec in zip(operands, in_specs)
            ]
        )

    return placed


class Ring:
    def __init__(self):
        self.count = lax.axis_size("tensor")
        self.sections = lax.axis_size("section")
        self.direct = self.count <= DIRECT_PEERS
        me = lax.axis_index("tensor")
        order = jnp.arange(self.count, dtype=jnp.int32)
        self.sources = (me - order) % self.count if self.direct else order

    def send(self, value, origin, target, step):
        n, m = self.count, self.sections
        perm = [(t * m + origin, (t + step) % n * m + target) for t in range(n)]
        return lax.ppermute(value, ("tensor", "section"), perm)

    def advance(self, value, origin, target):
        if self.direct:
            return [self.send(value, origin, target, step) for step in range(self.count)]
        value = lax.ppermute(value, "section", [(origin, target)])
        whole = lax.all_gather(value, "tensor", axis=0, tiled=False)
        return [whole[slot] for slot in range(self.count)]

    def trade(self, values):
        return lax.all_to_all(values, "tensor", split_axis=0, concat_axis=0, tiled=True)


def pack_kernel(info, tensor_ref, table, context, pool, hidden, out):
    n, heads_dev, group, kv_heads, width, page_len, extra = info
    tokens = pool.shape[0]
    pages = tokens // page_len
    row_dev, blocks = table.shape
    lane = lax.broadcasted_iota(jnp.int32, (extra, 2 * width), 1)
    row = lax.broadcasted_iota(jnp.int32, (extra, 2 * width), 0)
    first = tensor_ref[0] * pages
    aux = jnp.zeros((extra, 2 * width), jnp.float32)
    for j in range(row_dev):
        length = context[j]
        uses = jnp.zeros((extra, 2 * width), jnp.float32)
        for b in range(blocks):
            offset = lane - (table[j, b] - first) * page_len
            inside = (offset >= 0) & (offset < page_len) & (offset + b * page_len < length)
            uses = uses + jnp.where(inside, 1.0, 0.0)
        aux = jnp.where(row == j, uses, aux)
        aux = jnp.where(row == row_dev + j, length.astype(jnp.float32), aux)
    aux = aux.astype(jnp.bfloat16)
    rows, slice_len = hidden.shape
    strips = slice_len // (2 * width)
    stream = hidden[...]
    stream = [stream[:, c * 2 * width : (c + 1) * 2 * width] for c in range(strips)]
    stream = jnp.concatenate(stream, axis=0)
    for k in range(n):
        head = k * heads_dev // group * HD
        out[k, 0:tokens, 0:width] = pool[:, head : head + width]
        head = head + kv_heads * HD
        out[k, 0:tokens, width : 2 * width] = pool[:, head : head + width]
        out[k, tokens : tokens + extra, :] = aux
        out[k, tokens + extra :, :] = stream


def unpack_kernel(info, frequency, packs, counts, cosine, sine, wide, lengths):
    n, row_dev, tokens, extra = info
    counts[...] = jnp.zeros_like(counts)
    rows, features = wide.shape
    slice_len = features // n
    strip = packs.shape[2]
    for k in range(n):
        aux = packs[k, tokens : tokens + extra, :].astype(jnp.float32)
        base = k * row_dev
        for j in range(row_dev):
            counts[k, base + j : base + j + 1, :] = aux[j : j + 1, :tokens]
            lengths[base + j : base + j + 1, :] = aux[row_dev + j : row_dev + j + 1, :HD]
        for c in range(slice_len // strip):
            at = tokens + extra + c * rows
            to = k * slice_len + c * strip
            wide[:, to : to + strip] = packs[k, at : at + rows, :]
    angles = lengths[...] * frequency[...]
    lane = lax.broadcasted_iota(jnp.int32, angles.shape, 1)
    cosine[...] = jnp.cos(angles)
    sine[...] = jnp.where(lane < HD // 2, -1.0, 1.0) * jnp.sin(angles)


def rotate(values, cosine, sine):
    swapped = jnp.concatenate([values[:, HD // 2 :], values[:, : HD // 2]], axis=1)
    return values * cosine + swapped * sine


def project_kernel(info, sources, gain, wq, wkv, bias, counts, cosine, sine, *refs):
    n, heads_dev, group, tokens, width = info
    packs, *pieces, out = refs
    features = gain.shape[1]
    slice_len = features // n
    if len(pieces) == n:
        wide = [piece[...].astype(jnp.float32) for piece in pieces]
        starts = [pl.multiple_of(sources[k] * slice_len, HD) for k in range(n)]
    else:
        starts = [k * slice_len for k in range(n)]
        wide = [pieces[0][:, at : at + slice_len].astype(jnp.float32) for at in starts]
    total = functools.reduce(
        jnp.add, [jnp.sum(value * value, axis=1, keepdims=True) for value in wide]
    )
    inverse = lax.rsqrt(total * (1.0 / features) + epsilon)
    queries = None
    for k in range(n):
        at = starts[k]
        scale = gain[:, pl.ds(at, slice_len)].astype(jnp.float32)
        normed = (wide[k] * inverse * scale).astype(jnp.bfloat16)
        q_part = jnp.dot(normed, wq[pl.ds(at, slice_len), :], preferred_element_type=jnp.float32)
        kv_part = jnp.dot(normed, wkv[pl.ds(at, slice_len), :], preferred_element_type=jnp.float32)
        queries = q_part if queries is None else queries + q_part
        fresh = kv_part if k == 0 else fresh + kv_part
    queries = (queries + bias[...].astype(jnp.float32)).astype(jnp.bfloat16).astype(jnp.float32)
    span = heads_dev * HD
    out[0, :, 3 * span : 3 * span + fresh.shape[1]] = fresh.astype(jnp.bfloat16).astype(jnp.float32)
    for i in range(heads_dev):
        head = slice(i * HD, (i + 1) * HD)
        rotated = rotate(queries[:, head], cosine[...], sine[...]).astype(jnp.bfloat16)
        key_at = (i // group) * HD
        scores = []
        for k in range(n):
            keys = packs[k, 0:tokens, key_at : key_at + HD]
            scores.append(
                lax.dot_general(
                    rotated, keys, (((1,), (1,)), ((), ())), preferred_element_type=jnp.float32
                )
                * HD ** (-0.5)
            )
        tops = [
            jnp.where(counts[k] > 0.0, scores[k], -1e30) for k in range(n)
        ]
        top = functools.reduce(
            jnp.maximum, [jnp.max(value, axis=1, keepdims=True) for value in tops]
        )
        mass = 0.0
        mixed = 0.0
        for k in range(n):
            weight = counts[k] * jnp.exp(tops[k] - top)
            mass = mass + jnp.sum(weight, axis=1, keepdims=True)
            values = packs[k, 0:tokens, width + key_at : width + key_at + HD]
            mixed = mixed + jnp.dot(
                weight.astype(jnp.bfloat16), values, preferred_element_type=jnp.float32
            )
        out[0, :, i * HD : (i + 1) * HD] = rotated.astype(jnp.float32)
        out[0, :, span + i * HD : span + (i + 1) * HD] = mixed / mass
        out[0, :, 2 * span + i * HD : 2 * span + (i + 1) * HD] = jnp.broadcast_to(
            top + jnp.log(mass), (mixed.shape[0], HD)
        )
    for k in range(1, n):
        out[k] = out[0]


def output_kernel(info, own, wout, cosine, sine, slots, *refs):
    n, heads_dev, group, kv_heads, kv_width, splits = info
    outs = refs[:splits]
    fresh = refs[splits]
    span = heads_dev * HD
    for j in range(n):
        fresh[:, j * kv_width : (j + 1) * kv_width] = slots[j, :, 3 * span : 3 * span + kv_width]
    keys = []
    for h in range(kv_heads):
        key = rotate(fresh[:, h * HD : (h + 1) * HD], cosine[...], sine[...])
        keys.append(key.astype(jnp.bfloat16).astype(jnp.float32))
    mixture = []
    for h in range(n * heads_dev):
        j, i = divmod(h, heads_dev)
        kv = h // group
        query = slots[j, :, i * HD : (i + 1) * HD]
        cached = slots[j, :, span + i * HD : span + (i + 1) * HD]
        level = slots[j, :, 2 * span + i * HD : 2 * span + (i + 1) * HD]
        value = fresh[:, (kv_heads + kv) * HD : (kv_heads + kv + 1) * HD]
        score = jnp.sum(query * keys[kv], axis=1, keepdims=True) * HD ** (-0.5)
        weight = 1.0 / (1.0 + jnp.exp(level - score))
        mixture.append((cached + weight * (value - cached)).astype(jnp.bfloat16))
    mixture = jnp.concatenate(mixture, axis=1)
    stream = own[...].astype(jnp.float32) + jnp.dot(
        mixture, wout[...], preferred_element_type=jnp.float32
    )
    stream = stream.astype(jnp.bfloat16)
    rows = stream.shape[0] // splits
    for part in range(splits):
        outs[part][...] = stream[part * rows : (part + 1) * rows]


def shards(
    hidden,
    norm_gain,
    query_weight,
    query_bias,
    kv_weight,
    out_weight,
    kv_pool,
    page_table,
    context_len,
):
    ring = Ring()
    n = ring.count
    sections = ring.sections
    section_id = lax.axis_index("section")
    tensor_id = lax.axis_index("tensor")
    rows, slice_len = hidden.shape
    row_dev = page_table.shape[0]
    page_len = kv_pool.shape[2]
    tokens = kv_pool.shape[1] * page_len
    wq, wkv, wout = query_weight[0], kv_weight[0], out_weight[0]
    heads_dev = wq.shape[1] // HD
    kv_width = wkv.shape[1]
    kv_heads = kv_pool.shape[3] // (2 * HD)
    group = heads_dev * n // kv_heads
    width = max(1, heads_dev // group) * HD
    f32, bf16 = jnp.float32, jnp.bfloat16

    extra = round_up(2 * row_dev, 16)
    pack_info = (n, heads_dev, group, kv_heads, width, page_len, extra)
    height = tokens + extra + rows * slice_len // (2 * width)
    packs = kernel_call(
        functools.partial(pack_kernel, pack_info),
        [jax.ShapeDtypeStruct((n, height, 2 * width), bf16)],
        [SMEM] * 3 + [VMEM] * 2,
        many=False,
    )(
        tensor_id.reshape(1),
        page_table,
        context_len,
        kv_pool.reshape(tokens, kv_pool.shape[3]),
        hidden,
    )
    packs = ring.trade(packs)
    frequency = rope_base ** (-(jnp.arange(HD // 2, dtype=f32) * 2.0) / HD)
    frequency = jnp.concatenate([frequency, frequency])[None, :]
    counts, cosine, sine, first = kernel_call(
        functools.partial(unpack_kernel, (n, row_dev, tokens, extra)),
        [
            jax.ShapeDtypeStruct((n, rows, tokens), f32),
            jax.ShapeDtypeStruct((rows, HD), f32),
            jax.ShapeDtypeStruct((rows, HD), f32),
            jax.ShapeDtypeStruct((rows, n * slice_len), bf16),
        ],
        [VMEM] * 2,
        [pltpu.VMEM((rows, HD), f32)],
    )(frequency, packs)

    message = 3 * heads_dev * HD + round_up(kv_width, HD)
    pieces = [first]
    own = hidden
    for layer in range(sections):
        sent = kernel_call(
            functools.partial(project_kernel, (n, heads_dev, group, tokens, width)),
            [jax.ShapeDtypeStruct((n, rows, message), f32)],
            [SMEM] + [VMEM] * (8 + len(pieces)),
            many=False,
        )(ring.sources, norm_gain, wq, wkv, query_bias, counts, cosine, sine, packs, *pieces)
        parts = ring.trade(sent)
        splits = sections if layer == sections - 1 else 1
        stream = kernel_call(
            functools.partial(
                output_kernel, (n, heads_dev, group, kv_heads, kv_width, splits)
            ),
            [jax.ShapeDtypeStruct((rows // splits, slice_len), bf16)] * splits,
            [VMEM] * 5,
            [pltpu.VMEM((rows, n * kv_width), f32)],
        )(own, wout, cosine, sine, parts)
        if layer < sections - 1:
            pieces = ring.advance(stream[0], layer, layer + 1)
            own = pieces[0] if ring.direct else pieces_own(pieces, tensor_id)
    last = sections - 1
    result = jnp.where(section_id == last, stream[last], jnp.zeros_like(stream[last]))
    for target in range(last):
        result = result + lax.ppermute(stream[target], "section", [(last, target)])
    return result


def pieces_own(pieces, tensor_id):
    return lax.dynamic_index_in_dim(jnp.stack(pieces), tensor_id, 0, keepdims=False)


def solution(mesh):
    return jax.shard_map(
        shards,
        mesh=mesh,
        in_specs=(
            P("groups", "tensor"),
            P("section", None),
            P("section", None, "tensor"),
            P("section", "tensor"),
            P("section", None, "tensor"),
            P("section", None, "tensor"),
            P("section", ("groups", "tensor"), None, None),
            P(("groups", "tensor"), None),
            P(("groups", "tensor")),
        ),
        out_specs=P(("groups", "section"), "tensor"),
        check_vma=False,
    )
```

```python
import functools

import jax
import jax.numpy as jnp
import numpy as np
from jax import lax
from jax.experimental import pallas as pl
from jax.experimental.pallas import tpu as pltpu
from jax.sharding import PartitionSpec as P

HD = 128
epsilon = 1e-06
rope_base = 1000000.0
DIRECT_PEERS = 8
KERNEL_VMEM = 24 * 2**20
VMEM = pl.BlockSpec(memory_space=pltpu.VMEM)
SMEM = pl.BlockSpec(memory_space=pltpu.SMEM)


def round_up(value, unit):
    return -(-value // unit) * unit


def kernel_call(body, outs, in_specs, scratch=(), many=True, place=True):
    specs = [VMEM] * len(outs)
    call = pl.pallas_call(
        body,
        out_shape=outs if many else outs[0],
        in_specs=in_specs,
        out_specs=specs if many else specs[0],
        scratch_shapes=list(scratch),
        compiler_params=pltpu.CompilerParams(vmem_limit_bytes=KERNEL_VMEM),
    )

    def placed(*operands):
        put = pltpu.with_memory_space_constraint
        if not place:
            return call(*[put(value, pltpu.HBM) for value in operands])
        return call(
            *[
                put(value, pltpu.VMEM) if spec is VMEM else value
                for value, spec in zip(operands, in_specs)
            ]
        )

    return placed


class Ring:
    def __init__(self):
        self.count = lax.axis_size("tensor")
        self.sections = lax.axis_size("section")
        self.direct = self.count <= DIRECT_PEERS

    def send(self, value, origin, target, step):
        n, m = self.count, self.sections
        perm = [(t * m + origin, (t + step) % n * m + target) for t in range(n)]
        return lax.ppermute(value, ("tensor", "section"), perm)

    def advance(self, value, origin, target):
        if self.direct:
            return [self.send(value, origin, target, step) for step in range(self.count)]
        value = lax.ppermute(value, "section", [(origin, target)])
        return [lax.all_gather(value, "tensor", axis=1, tiled=True)]

    def trade(self, values):
        return lax.all_to_all(values, "tensor", split_axis=0, concat_axis=0, tiled=True)


def load_kernel(*refs):
    count = len(refs) // 2 - 1
    sources, outs, arrived = refs[:count], refs[count + 1 : -1], refs[-1]
    copies = [
        pltpu.make_async_copy(sources[i], outs[i], arrived.at[i]) for i in range(count)
    ]
    for copy in copies:
        copy.start()
    for copy in copies:
        copy.wait()


def load(values, after):
    hbm = pl.BlockSpec(memory_space=pltpu.HBM)
    return pl.pallas_call(
        load_kernel,
        out_shape=[pltpu.VMEM(value.shape, value.dtype) for value in values],
        in_specs=[hbm] * (len(values) + 1),
        out_specs=[VMEM] * len(values),
        scratch_shapes=[pltpu.SemaphoreType.DMA((len(values),))],
        compiler_params=pltpu.CompilerParams(vmem_limit_bytes=KERNEL_VMEM),
    )(*[pltpu.with_memory_space_constraint(value, pltpu.HBM) for value in values], after)


def pack_kernel(info, tensor_ref, table, context, pool, hidden, out):
    n, heads_dev, group, kv_heads, width, page_len, extra = info
    tokens = pool.shape[0]
    pages = tokens // page_len
    row_dev, blocks = table.shape
    lane = lax.broadcasted_iota(jnp.int32, (extra, 2 * width), 1)
    row = lax.broadcasted_iota(jnp.int32, (extra, 2 * width), 0)
    first = tensor_ref[0] * pages
    aux = jnp.zeros((extra, 2 * width), jnp.float32)
    for j in range(row_dev):
        length = context[j]
        uses = jnp.zeros((extra, 2 * width), jnp.float32)
        for b in range(blocks):
            offset = lane - (table[j, b] - first) * page_len
            inside = (offset >= 0) & (offset < page_len) & (offset + b * page_len < length)
            uses = uses + jnp.where(inside, 1.0, 0.0)
        aux = jnp.where(row == j, uses, aux)
        aux = jnp.where(row == row_dev + j, length.astype(jnp.float32), aux)
    aux = aux.astype(jnp.bfloat16)
    rows, slice_len = hidden.shape
    strips = slice_len // (2 * width)
    stream = hidden[...]
    stream = [stream[:, c * 2 * width : (c + 1) * 2 * width] for c in range(strips)]
    stream = jnp.concatenate(stream, axis=0)
    for k in range(n):
        head = k * heads_dev // group * HD
        out[k, 0:tokens, 0:width] = pool[:, head : head + width]
        head = head + kv_heads * HD
        out[k, 0:tokens, width : 2 * width] = pool[:, head : head + width]
        out[k, tokens : tokens + extra, :] = aux
        out[k, tokens + extra :, :] = stream


def unpack_kernel(info, frequency, packs, counts, cosine, sine, wide, lengths):
    n, row_dev, tokens, extra = info
    counts[...] = jnp.zeros_like(counts)
    rows, features = wide.shape
    slice_len = features // n
    strip = packs.shape[2]
    for k in range(n):
        aux = packs[k, tokens : tokens + extra, :].astype(jnp.float32)
        base = k * row_dev
        for j in range(row_dev):
            counts[k, base + j : base + j + 1, :] = aux[j : j + 1, :tokens]
            lengths[base + j : base + j + 1, :] = aux[row_dev + j : row_dev + j + 1, :HD]
        for c in range(slice_len // strip):
            at = tokens + extra + c * rows
            to = k * slice_len + c * strip
            wide[:, to : to + strip] = packs[k, at : at + rows, :]
    angles = lengths[...] * frequency[...]
    lane = lax.broadcasted_iota(jnp.int32, angles.shape, 1)
    cosine[...] = jnp.cos(angles)
    sine[...] = jnp.where(lane < HD // 2, -1.0, 1.0) * jnp.sin(angles)


def rotate(values, cosine, sine):
    swapped = jnp.concatenate([values[:, HD // 2 :], values[:, : HD // 2]], axis=1)
    return values * cosine + swapped * sine


def project_kernel(info, tensor_ref, gain, wq, wkv, bias, counts, cosine, sine, *refs):
    n, heads_dev, group, tokens, width, rotated_order = info
    packs, *pieces, out = refs
    features = gain.shape[1]
    slice_len = features // n
    if rotated_order:
        wide = [piece[...].astype(jnp.float32) for piece in pieces]
        me = tensor_ref[0]
        starts = [pl.multiple_of((me + n - k) % n * slice_len, HD) for k in range(n)]
    else:
        starts = [k * slice_len for k in range(n)]
        wide = [pieces[0][:, at : at + slice_len].astype(jnp.float32) for at in starts]
    total = functools.reduce(
        jnp.add, [jnp.sum(value * value, axis=1, keepdims=True) for value in wide]
    )
    inverse = lax.rsqrt(total * (1.0 / features) + epsilon)
    queries = None
    for k in range(n):
        at = starts[k]
        scale = gain[:, pl.ds(at, slice_len)].astype(jnp.float32)
        normed = (wide[k] * inverse * scale).astype(jnp.bfloat16)
        q_part = jnp.dot(normed, wq[pl.ds(at, slice_len), :], preferred_element_type=jnp.float32)
        kv_part = jnp.dot(normed, wkv[pl.ds(at, slice_len), :], preferred_element_type=jnp.float32)
        queries = q_part if queries is None else queries + q_part
        fresh = kv_part if k == 0 else fresh + kv_part
    queries = (queries + bias[...].astype(jnp.float32)).astype(jnp.bfloat16).astype(jnp.float32)
    span = heads_dev * HD
    out[0, :, 3 * span : 3 * span + fresh.shape[1]] = fresh.astype(jnp.bfloat16)
    for i in range(heads_dev):
        head = slice(i * HD, (i + 1) * HD)
        rotated = rotate(queries[:, head], cosine[...], sine[...]).astype(jnp.bfloat16)
        key_at = (i // group) * HD
        scores = []
        for k in range(n):
            keys = packs[k, 0:tokens, key_at : key_at + HD]
            scores.append(
                lax.dot_general(
                    rotated, keys, (((1,), (1,)), ((), ())), preferred_element_type=jnp.float32
                )
                * HD ** (-0.5)
            )
        tops = [
            jnp.where(counts[k] > 0.0, scores[k], -1e30) for k in range(n)
        ]
        top = functools.reduce(
            jnp.maximum, [jnp.max(value, axis=1, keepdims=True) for value in tops]
        )
        mass = 0.0
        mixed = 0.0
        for k in range(n):
            weight = counts[k] * jnp.exp(tops[k] - top)
            mass = mass + jnp.sum(weight, axis=1, keepdims=True)
            values = packs[k, 0:tokens, width + key_at : width + key_at + HD]
            mixed = mixed + jnp.dot(
                weight.astype(jnp.bfloat16), values, preferred_element_type=jnp.float32
            )
        out[0, :, i * HD : (i + 1) * HD] = rotated
        out[0, :, span + i * HD : span + (i + 1) * HD] = (mixed / mass).astype(
            jnp.bfloat16
        )
        level = jnp.broadcast_to(top + jnp.log(mass), (mixed.shape[0], HD))
        lane = lax.broadcasted_iota(jnp.int32, level.shape, 1)
        upper = level.astype(jnp.bfloat16).astype(jnp.float32)
        middle = (level - upper).astype(jnp.bfloat16).astype(jnp.float32)
        lower = level - upper - middle
        terms = jnp.where(lane == 0, upper, jnp.where(lane == 1, middle, lower))
        terms = jnp.where(lane < 3, terms, 0.0).astype(jnp.bfloat16)
        out[0, :, 2 * span + i * HD : 2 * span + (i + 1) * HD] = terms
    for k in range(1, n):
        out[k] = out[0]


def output_kernel(info, own, wout, cosine, sine, slots, *refs):
    n, heads_dev, group, kv_heads, kv_width, splits = info
    outs = refs[:splits]
    fresh = refs[splits]
    span = heads_dev * HD
    for j in range(n):
        fresh[:, j * kv_width : (j + 1) * kv_width] = slots[
            j, :, 3 * span : 3 * span + kv_width
        ].astype(jnp.float32)
    keys = []
    for h in range(kv_heads):
        key = rotate(fresh[:, h * HD : (h + 1) * HD], cosine[...], sine[...])
        keys.append(key.astype(jnp.bfloat16).astype(jnp.float32))
    mixture = []
    for h in range(n * heads_dev):
        j, i = divmod(h, heads_dev)
        kv = h // group
        query = slots[j, :, i * HD : (i + 1) * HD].astype(jnp.float32)
        cached = slots[j, :, span + i * HD : span + (i + 1) * HD].astype(jnp.float32)
        terms = slots[j, :, 2 * span + i * HD : 2 * span + (i + 1) * HD]
        level = jnp.sum(terms.astype(jnp.float32), axis=1, keepdims=True)
        value = fresh[:, (kv_heads + kv) * HD : (kv_heads + kv + 1) * HD]
        score = jnp.sum(query * keys[kv], axis=1, keepdims=True) * HD ** (-0.5)
        weight = 1.0 / (1.0 + jnp.exp(level - score))
        mixture.append((cached + weight * (value - cached)).astype(jnp.bfloat16))
    mixture = jnp.concatenate(mixture, axis=1)
    stream = own[...].astype(jnp.float32) + jnp.dot(
        mixture, wout[...], preferred_element_type=jnp.float32
    )
    stream = stream.astype(jnp.bfloat16)
    rows = stream.shape[0] // splits
    for part in range(splits):
        outs[part][...] = stream[part * rows : (part + 1) * rows]


def shards(
    hidden,
    norm_gain,
    query_weight,
    query_bias,
    kv_weight,
    out_weight,
    kv_pool,
    page_table,
    context_len,
):
    ring = Ring()
    n = ring.count
    sections = ring.sections
    section_id = lax.axis_index("section")
    tensor_id = lax.axis_index("tensor")
    rows, slice_len = hidden.shape
    row_dev = page_table.shape[0]
    page_len = kv_pool.shape[2]
    tokens = kv_pool.shape[1] * page_len
    wq, wkv, wout = query_weight[0], kv_weight[0], out_weight[0]
    heads_dev = wq.shape[1] // HD
    kv_width = wkv.shape[1]
    kv_heads = kv_pool.shape[3] // (2 * HD)
    group = heads_dev * n // kv_heads
    width = max(1, heads_dev // group) * HD
    f32, bf16 = jnp.float32, jnp.bfloat16

    extra = round_up(2 * row_dev, 16)
    pack_info = (n, heads_dev, group, kv_heads, width, page_len, extra)
    height = tokens + extra + rows * slice_len // (2 * width)
    packs = kernel_call(
        functools.partial(pack_kernel, pack_info),
        [jax.ShapeDtypeStruct((n, height, 2 * width), bf16)],
        [SMEM] * 3 + [VMEM] * 2,
        many=False,
        place=False,
    )(
        tensor_id.reshape(1),
        page_table,
        context_len,
        kv_pool.reshape(tokens, kv_pool.shape[3]),
        hidden,
    )
    wout, gain, bias = load((wout, norm_gain, query_bias), packs)
    packs = ring.trade(packs)
    frequency = np.float32(rope_base) ** (-(np.arange(HD // 2, dtype=np.float32) * 2.0) / HD)
    frequency = np.concatenate([frequency, frequency])[None, :].astype(np.float32)
    counts, cosine, sine, first = kernel_call(
        functools.partial(unpack_kernel, (n, row_dev, tokens, extra)),
        [
            jax.ShapeDtypeStruct((n, rows, tokens), f32),
            jax.ShapeDtypeStruct((rows, HD), f32),
            jax.ShapeDtypeStruct((rows, HD), f32),
            jax.ShapeDtypeStruct((rows, n * slice_len), bf16),
        ],
        [VMEM] * 2,
        [pltpu.VMEM((rows, HD), f32)],
    )(frequency, packs)

    message = 3 * heads_dev * HD + round_up(kv_width, HD)
    project_info = (n, heads_dev, group, tokens, width)
    pieces = [first]
    own = hidden
    for layer in range(sections):
        sent = kernel_call(
            functools.partial(project_kernel, project_info + (ring.direct and layer > 0,)),
            [jax.ShapeDtypeStruct((n, rows, message), bf16)],
            [SMEM] + [VMEM] * (8 + len(pieces)),
            many=False,
        )(tensor_id.reshape(1), gain, wq, wkv, bias, counts, cosine, sine, packs, *pieces)
        parts = ring.trade(sent)
        splits = sections if layer == sections - 1 else 1
        stream = kernel_call(
            functools.partial(
                output_kernel, (n, heads_dev, group, kv_heads, kv_width, splits)
            ),
            [jax.ShapeDtypeStruct((rows // splits, slice_len), bf16)] * splits,
            [VMEM] * 5,
            [pltpu.VMEM((rows, n * kv_width), f32)],
        )(own, wout, cosine, sine, parts)
        if layer < sections - 1:
            pieces = ring.advance(stream[0], layer, layer + 1)
            own = pieces[0] if ring.direct else own_slice(pieces[0], tensor_id, slice_len)
    last = sections - 1
    result = jnp.where(section_id == last, stream[last], jnp.zeros_like(stream[last]))
    for target in range(last):
        result = result + lax.ppermute(stream[target], "section", [(last, target)])
    return result


def own_slice(whole, tensor_id, slice_len):
    return lax.dynamic_slice_in_dim(whole, tensor_id * slice_len, slice_len, axis=1)


def solution(mesh):
    return jax.shard_map(
        shards,
        mesh=mesh,
        in_specs=(
            P("groups", "tensor"),
            P("section", None),
            P("section", None, "tensor"),
            P("section", "tensor"),
            P("section", None, "tensor"),
            P("section", None, "tensor"),
            P("section", ("groups", "tensor"), None, None),
            P(("groups", "tensor"), None),
            P(("groups", "tensor")),
        ),
        out_specs=P(("groups", "section"), "tensor"),
        check_vma=False,
    )
```

```python
import functools

import jax
import jax.numpy as jnp
import numpy as np
from jax import lax
from jax.experimental import pallas as pl
from jax.experimental.pallas import tpu as pltpu
from jax.sharding import PartitionSpec as P

HD = 128
epsilon = 1e-06
rope_base = 1000000.0
DIRECT_PEERS = 8
KERNEL_VMEM = 24 * 2**20
VMEM = pl.BlockSpec(memory_space=pltpu.VMEM)
SMEM = pl.BlockSpec(memory_space=pltpu.SMEM)


def round_up(value, unit):
    return -(-value // unit) * unit


def kernel_call(body, outs, in_specs, scratch=(), many=True, place=True):
    specs = [VMEM] * len(outs)
    call = pl.pallas_call(
        body,
        out_shape=outs if many else outs[0],
        in_specs=in_specs,
        out_specs=specs if many else specs[0],
        scratch_shapes=list(scratch),
        compiler_params=pltpu.CompilerParams(vmem_limit_bytes=KERNEL_VMEM),
    )

    def placed(*operands):
        put = pltpu.with_memory_space_constraint
        if not place:
            return call(*[put(value, pltpu.HBM) for value in operands])
        return call(
            *[
                put(value, pltpu.VMEM) if spec is VMEM else value
                for value, spec in zip(operands, in_specs)
            ]
        )

    return placed


class Ring:
    def __init__(self):
        self.count = lax.axis_size("tensor")
        self.sections = lax.axis_size("section")
        self.direct = self.count <= DIRECT_PEERS
        far = sorted(range(1, self.count), key=lambda step: -max(step, self.count - step))
        self.steps = tuple(far) + (0,)

    def send(self, value, origin, target, step):
        n, m = self.count, self.sections
        perm = [(t * m + origin, (t + step) % n * m + target) for t in range(n)]
        return lax.ppermute(value, ("tensor", "section"), perm)

    def advance(self, value, origin, target):
        if self.direct:
            return [self.send(value, origin, target, step) for step in self.steps]
        value = lax.ppermute(value, "section", [(origin, target)])
        return [lax.all_gather(value, "tensor", axis=1, tiled=True)]

    def trade(self, values):
        return lax.all_to_all(values, "tensor", split_axis=0, concat_axis=0, tiled=True)


def load_kernel(*refs):
    count = len(refs) // 2 - 1
    sources, outs, arrived = refs[:count], refs[count + 1 : -1], refs[-1]
    copies = [
        pltpu.make_async_copy(sources[i], outs[i], arrived.at[i]) for i in range(count)
    ]
    for copy in copies:
        copy.start()
    for copy in copies:
        copy.wait()


def load(values, after):
    hbm = pl.BlockSpec(memory_space=pltpu.HBM)
    return pl.pallas_call(
        load_kernel,
        out_shape=[pltpu.VMEM(value.shape, value.dtype) for value in values],
        in_specs=[hbm] * (len(values) + 1),
        out_specs=[VMEM] * len(values),
        scratch_shapes=[pltpu.SemaphoreType.DMA((len(values),))],
        compiler_params=pltpu.CompilerParams(vmem_limit_bytes=KERNEL_VMEM),
    )(*[pltpu.with_memory_space_constraint(value, pltpu.HBM) for value in values], after)


def pack_kernel(info, tensor_ref, table, context, pool, hidden, out):
    n, heads_dev, group, kv_heads, width, page_len, extra = info
    tokens = pool.shape[0]
    pages = tokens // page_len
    row_dev, blocks = table.shape
    lane = lax.broadcasted_iota(jnp.int32, (extra, 2 * width), 1)
    row = lax.broadcasted_iota(jnp.int32, (extra, 2 * width), 0)
    first = tensor_ref[0] * pages
    aux = jnp.zeros((extra, 2 * width), jnp.float32)
    for j in range(row_dev):
        length = context[j]
        uses = jnp.zeros((extra, 2 * width), jnp.float32)
        for b in range(blocks):
            offset = lane - (table[j, b] - first) * page_len
            inside = (offset >= 0) & (offset < page_len) & (offset + b * page_len < length)
            uses = uses + jnp.where(inside, 1.0, 0.0)
        aux = jnp.where(row == j, uses, aux)
        aux = jnp.where(row == row_dev + j, length.astype(jnp.float32), aux)
    aux = aux.astype(jnp.bfloat16)
    rows, slice_len = hidden.shape
    strips = slice_len // (2 * width)
    stream = hidden[...]
    stream = [stream[:, c * 2 * width : (c + 1) * 2 * width] for c in range(strips)]
    stream = jnp.concatenate(stream, axis=0)
    for k in range(n):
        head = k * heads_dev // group * HD
        out[k, 0:tokens, 0:width] = pool[:, head : head + width]
        head = head + kv_heads * HD
        out[k, 0:tokens, width : 2 * width] = pool[:, head : head + width]
        out[k, tokens : tokens + extra, :] = aux
        out[k, tokens + extra :, :] = stream


def unpack_kernel(info, frequency, packs, counts, cosine, sine, wide, lengths):
    n, row_dev, tokens, extra = info
    counts[...] = jnp.zeros_like(counts)
    rows, features = wide.shape
    slice_len = features // n
    strip = packs.shape[2]
    for k in range(n):
        aux = packs[k, tokens : tokens + extra, :].astype(jnp.float32)
        base = k * row_dev
        for j in range(row_dev):
            counts[k, base + j : base + j + 1, :] = aux[j : j + 1, :tokens]
            lengths[base + j : base + j + 1, :] = aux[row_dev + j : row_dev + j + 1, :HD]
        for c in range(slice_len // strip):
            at = tokens + extra + c * rows
            to = k * slice_len + c * strip
            wide[:, to : to + strip] = packs[k, at : at + rows, :]
    angles = lengths[...] * frequency[...]
    lane = lax.broadcasted_iota(jnp.int32, angles.shape, 1)
    cosine[...] = jnp.cos(angles)
    sine[...] = jnp.where(lane < HD // 2, -1.0, 1.0) * jnp.sin(angles)


def rotate(values, cosine, sine):
    swapped = jnp.concatenate([values[:, HD // 2 :], values[:, : HD // 2]], axis=1)
    return values * cosine + swapped * sine


def project_kernel(info, tensor_ref, gain, wq, wkv, bias, counts, cosine, sine, *refs):
    n, heads_dev, group, tokens, width, steps = info
    packs, *pieces, out = refs
    features = gain.shape[1]
    slice_len = features // n
    if steps:
        wide = [piece[...].astype(jnp.float32) for piece in pieces]
        me = tensor_ref[0]
        starts = [pl.multiple_of((me + n - step) % n * slice_len, HD) for step in steps]
    else:
        starts = [k * slice_len for k in range(n)]
        wide = [pieces[0][:, at : at + slice_len].astype(jnp.float32) for at in starts]
    total = functools.reduce(
        jnp.add, [jnp.sum(value * value, axis=1, keepdims=True) for value in wide]
    )
    inverse = lax.rsqrt(total * (1.0 / features) + epsilon)
    queries = None
    for k in range(n):
        at = starts[k]
        scale = gain[:, pl.ds(at, slice_len)].astype(jnp.float32)
        normed = (wide[k] * inverse * scale).astype(jnp.bfloat16)
        q_part = jnp.dot(normed, wq[pl.ds(at, slice_len), :], preferred_element_type=jnp.float32)
        kv_part = jnp.dot(normed, wkv[pl.ds(at, slice_len), :], preferred_element_type=jnp.float32)
        queries = q_part if queries is None else queries + q_part
        fresh = kv_part if k == 0 else fresh + kv_part
    queries = (queries + bias[...].astype(jnp.float32)).astype(jnp.bfloat16).astype(jnp.float32)
    span = heads_dev * HD
    out[0, :, 3 * span : 3 * span + fresh.shape[1]] = fresh.astype(jnp.bfloat16)
    for i in range(heads_dev):
        head = slice(i * HD, (i + 1) * HD)
        rotated = rotate(queries[:, head], cosine[...], sine[...]).astype(jnp.bfloat16)
        key_at = (i // group) * HD
        scores = []
        for k in range(n):
            keys = packs[k, 0:tokens, key_at : key_at + HD]
            scores.append(
                lax.dot_general(
                    rotated, keys, (((1,), (1,)), ((), ())), preferred_element_type=jnp.float32
                )
                * HD ** (-0.5)
            )
        tops = [
            jnp.where(counts[k] > 0.0, scores[k], -1e30) for k in range(n)
        ]
        top = functools.reduce(
            jnp.maximum, [jnp.max(value, axis=1, keepdims=True) for value in tops]
        )
        mass = 0.0
        mixed = 0.0
        for k in range(n):
            weight = counts[k] * jnp.exp(tops[k] - top)
            mass = mass + jnp.sum(weight, axis=1, keepdims=True)
            values = packs[k, 0:tokens, width + key_at : width + key_at + HD]
            mixed = mixed + jnp.dot(
                weight.astype(jnp.bfloat16), values, preferred_element_type=jnp.float32
            )
        out[0, :, i * HD : (i + 1) * HD] = rotated
        out[0, :, span + i * HD : span + (i + 1) * HD] = (mixed / mass).astype(
            jnp.bfloat16
        )
        level = jnp.broadcast_to(top + jnp.log(mass), (mixed.shape[0], HD))
        lane = lax.broadcasted_iota(jnp.int32, level.shape, 1)
        upper = level.astype(jnp.bfloat16).astype(jnp.float32)
        middle = (level - upper).astype(jnp.bfloat16).astype(jnp.float32)
        lower = level - upper - middle
        terms = jnp.where(lane == 0, upper, jnp.where(lane == 1, middle, lower))
        terms = jnp.where(lane < 3, terms, 0.0).astype(jnp.bfloat16)
        out[0, :, 2 * span + i * HD : 2 * span + (i + 1) * HD] = terms
    for k in range(1, n):
        out[k] = out[0]


def output_kernel(info, own, wout, cosine, sine, slots, *refs):
    n, heads_dev, group, kv_heads, kv_width, splits = info
    outs = refs[:splits]
    fresh = refs[splits]
    span = heads_dev * HD
    for j in range(n):
        fresh[:, j * kv_width : (j + 1) * kv_width] = slots[
            j, :, 3 * span : 3 * span + kv_width
        ].astype(jnp.float32)
    keys = []
    for h in range(kv_heads):
        key = rotate(fresh[:, h * HD : (h + 1) * HD], cosine[...], sine[...])
        keys.append(key.astype(jnp.bfloat16).astype(jnp.float32))
    mixture = []
    for h in range(n * heads_dev):
        j, i = divmod(h, heads_dev)
        kv = h // group
        query = slots[j, :, i * HD : (i + 1) * HD].astype(jnp.float32)
        cached = slots[j, :, span + i * HD : span + (i + 1) * HD].astype(jnp.float32)
        terms = slots[j, :, 2 * span + i * HD : 2 * span + (i + 1) * HD]
        level = jnp.sum(terms.astype(jnp.float32), axis=1, keepdims=True)
        value = fresh[:, (kv_heads + kv) * HD : (kv_heads + kv + 1) * HD]
        score = jnp.sum(query * keys[kv], axis=1, keepdims=True) * HD ** (-0.5)
        weight = 1.0 / (1.0 + jnp.exp(level - score))
        mixture.append((cached + weight * (value - cached)).astype(jnp.bfloat16))
    mixture = jnp.concatenate(mixture, axis=1)
    stream = own[...].astype(jnp.float32) + jnp.dot(
        mixture, wout[...], preferred_element_type=jnp.float32
    )
    stream = stream.astype(jnp.bfloat16)
    rows = stream.shape[0] // splits
    for part in range(splits):
        outs[part][...] = stream[part * rows : (part + 1) * rows]


def shards(
    hidden,
    norm_gain,
    query_weight,
    query_bias,
    kv_weight,
    out_weight,
    kv_pool,
    page_table,
    context_len,
):
    ring = Ring()
    n = ring.count
    sections = ring.sections
    section_id = lax.axis_index("section")
    tensor_id = lax.axis_index("tensor")
    rows, slice_len = hidden.shape
    row_dev = page_table.shape[0]
    page_len = kv_pool.shape[2]
    tokens = kv_pool.shape[1] * page_len
    wq, wkv, wout = query_weight[0], kv_weight[0], out_weight[0]
    heads_dev = wq.shape[1] // HD
    kv_width = wkv.shape[1]
    kv_heads = kv_pool.shape[3] // (2 * HD)
    group = heads_dev * n // kv_heads
    width = max(1, heads_dev // group) * HD
    f32, bf16 = jnp.float32, jnp.bfloat16

    extra = round_up(2 * row_dev, 16)
    pack_info = (n, heads_dev, group, kv_heads, width, page_len, extra)
    height = tokens + extra + rows * slice_len // (2 * width)
    packs = kernel_call(
        functools.partial(pack_kernel, pack_info),
        [jax.ShapeDtypeStruct((n, height, 2 * width), bf16)],
        [SMEM] * 3 + [VMEM] * 2,
        many=False,
        place=False,
    )(
        tensor_id.reshape(1),
        page_table,
        context_len,
        kv_pool.reshape(tokens, kv_pool.shape[3]),
        hidden,
    )
    wout, gain, bias = load((wout, norm_gain, query_bias), packs)
    packs = ring.trade(packs)
    frequency = np.float32(rope_base) ** (-(np.arange(HD // 2, dtype=np.float32) * 2.0) / HD)
    frequency = np.concatenate([frequency, frequency])[None, :].astype(np.float32)
    counts, cosine, sine, first = kernel_call(
        functools.partial(unpack_kernel, (n, row_dev, tokens, extra)),
        [
            jax.ShapeDtypeStruct((n, rows, tokens), f32),
            jax.ShapeDtypeStruct((rows, HD), f32),
            jax.ShapeDtypeStruct((rows, HD), f32),
            jax.ShapeDtypeStruct((rows, n * slice_len), bf16),
        ],
        [VMEM] * 2,
        [pltpu.VMEM((rows, HD), f32)],
    )(frequency, packs)

    message = 3 * heads_dev * HD + round_up(kv_width, HD)
    project_info = (n, heads_dev, group, tokens, width)
    pieces = [first]
    own = hidden
    order = ()
    for layer in range(sections):
        sent = kernel_call(
            functools.partial(project_kernel, project_info + (order,)),
            [jax.ShapeDtypeStruct((n, rows, message), bf16)],
            [SMEM] + [VMEM] * (8 + len(pieces)),
            many=False,
        )(tensor_id.reshape(1), gain, wq, wkv, bias, counts, cosine, sine, packs, *pieces)
        parts = ring.trade(sent)
        splits = sections if layer == sections - 1 else 1
        stream = kernel_call(
            functools.partial(
                output_kernel, (n, heads_dev, group, kv_heads, kv_width, splits)
            ),
            [jax.ShapeDtypeStruct((rows // splits, slice_len), bf16)] * splits,
            [VMEM] * 5,
            [pltpu.VMEM((rows, n * kv_width), f32)],
        )(own, wout, cosine, sine, parts)
        if layer < sections - 1:
            pieces = ring.advance(stream[0], layer, layer + 1)
            order = ring.steps if ring.direct else ()
            own = pieces[-1] if ring.direct else own_slice(pieces[0], tensor_id, slice_len)
    last = sections - 1
    result = jnp.where(section_id == last, stream[last], jnp.zeros_like(stream[last]))
    for target in range(last):
        result = result + lax.ppermute(stream[target], "section", [(last, target)])
    return result


def own_slice(whole, tensor_id, slice_len):
    return lax.dynamic_slice_in_dim(whole, tensor_id * slice_len, slice_len, axis=1)


def solution(mesh):
    return jax.shard_map(
        shards,
        mesh=mesh,
        in_specs=(
            P("groups", "tensor"),
            P("section", None),
            P("section", None, "tensor"),
            P("section", "tensor"),
            P("section", None, "tensor"),
            P("section", None, "tensor"),
            P("section", ("groups", "tensor"), None, None),
            P(("groups", "tensor"), None),
            P(("groups", "tensor")),
        ),
        out_specs=P(("groups", "section"), "tensor"),
        check_vma=False,
    )
```
